32 devices in a mesh: visit: 2 (over core), tx: 4 (over y, x), ty: 4 (over z).
Axes of the slice: x: 2, y: 2, z: 4, core: 2. Of those that a mesh axis runs over, the one named last changes fastest.
Arguments:
- raw: bfloat16 [4, 2048, 2048], P('visit', ('tx', 'ty')), may hold values from -12 to 12, as said below
- dark: float32 [2048, 2048], P(('tx', 'ty')), may hold values from 0 to 0.8
- flat: float32 [2048, 2048], P(('tx', 'ty')), may hold values from 0.5 to 1.5
- mask: int32 [4, 2048, 2048], P('visit', ('tx', 'ty')), may hold values 0 or 1
- offsets: int32 [4, 2], P('visit'), may hold values from 0 to 255
- scales: float32 [4, 2], P('visit'), may hold values from 0.985 to 1.015
- fracs: float32 [4, 2], P('visit'), may hold values from 0 to 1
Outputs:
- coadd: float32 [2048, 2048], P('visit', ('tx', 'ty'))
The draws below stay inside these ranges and needn't reach their ends.
Inputs may be any that keep to these rules, and one draw needn't show every extreme that they name: `raw`: each exposure's pixels have a noise level of its own.
All inputs are finite; a program needn't handle non-finite values. No bound on the sum of `mask` on one device may be relied on, other than what follows from the above.
Results may differ from the reference program's by a relative error of at most 0.00145.
The reference program's roundings to bfloat16 on the way count: a program that leaves them out, or rounds other values in their place, can miss the bound.
Values may be sent and summed in bfloat16 or wider, within the bound.
A program may use at most 64 MiB of HBM per device.

```python
import jax
import jax.numpy as jnp

P_SIZE = 2048
NEXP = 4
OFFSET = 256


def draw_raw(key, part):
    key_level = jax.random.fold_in(key, 11)
    key_noise = jax.random.fold_in(key, 12)
    levels = jnp.exp(jax.random.uniform(key_level, (NEXP, 1, 1), jnp.float32, jnp.log(0.5), jnp.log(2.0)))
    values = jnp.clip(jax.random.normal(key_noise, (NEXP, P_SIZE, P_SIZE), jnp.float32), -6.0, 6.0)
    return (values * levels).astype(jnp.bfloat16)


def place_ends(drawn, rng, smallest, top_value):
    longest = drawn.shape.index(max(drawn.shape))
    spots = []
    for shift in (0, 1):
        where = [jax.random.randint(jax.random.fold_in(rng, axis), (), 0, length) for axis, length in enumerate(drawn.shape)]
        where[longest] = (where[longest] + shift) % drawn.shape[longest]
        spots.append(tuple(where))
    return drawn.at[spots[0]].set(smallest).at[spots[1]].set(top_value)


def level_of(own_key, extent, split, smallest, top_value):
    loudness = 1.0
    for axis_at, blocks in split:
        steps = jax.random.uniform(jax.random.fold_in(jax.random.fold_in(own_key, 6), axis_at), (blocks,), jnp.float32, smallest / len(split), top_value / len(split))
        loudness = loudness * jnp.repeat(jnp.exp(steps), extent[axis_at] // blocks).reshape((-1,) + (1,) * (len(extent) - 1 - axis_at))
    return loudness


def setup_inputs(seed: int = 0) -> dict:
    keys = jax.random.split(jax.random.key(seed), 8)
    raw = draw_raw(jax.random.fold_in(keys[7], 71), 0)
    dark = jnp.clip(0.8 * jax.random.uniform(keys[1], (P_SIZE, P_SIZE), jnp.float32) ** level_of(keys[1], (P_SIZE, P_SIZE), ((0, 16),), -0.2, 0.2), 0.0, 0.8)
    flat = jnp.clip(1.0 + 0.1 * jax.random.normal(keys[2], (P_SIZE, P_SIZE), jnp.float32), 0.5, 1.5)
    mask = place_ends((jax.random.randint(keys[3], (NEXP, P_SIZE, P_SIZE), 0, 16) < 15).astype(jnp.int32), jax.random.fold_in(keys[3], 1), 0, 1)
    offsets = place_ends(jax.random.randint(keys[4], (NEXP, 2), 0, OFFSET), jax.random.fold_in(keys[4], 1), 0, OFFSET - 1).astype(jnp.int32)
    scales = jnp.clip(0.985 + 0.029999971 * jax.random.uniform(keys[5], (NEXP, 2), jnp.float32) ** level_of(keys[5], (NEXP, 2), ((0, 2),), -0.2, 0.2), 0.985, 1.015)
    fracs = jnp.clip(1.0 * jax.random.uniform(keys[6], (NEXP, 2), jnp.float32) ** level_of(keys[6], (NEXP, 2), ((0, 2),), -0.2, 0.2), 0.0, 1.0)
    return {"raw": raw, "dark": dark, "flat": flat, "mask": mask, "offsets": offsets, "scales": scales, "fracs": fracs}


def lanczos(offsets_t):
    return jnp.where(jnp.abs(offsets_t) < 3.0, jnp.sinc(offsets_t) * jnp.sinc(offsets_t / 3.0), 0.0)


def warp_last(image, offset, scale, frac):
    sky = jnp.arange(P_SIZE, dtype=jnp.float32)
    coords = (sky - offset.astype(jnp.float32)) * scale + frac
    base = jnp.floor(coords).astype(jnp.int32)
    total = jnp.zeros(image.shape, jnp.float32)
    for step in range(-2, 4):
        index = base + step
        taps = lanczos(coords - index.astype(jnp.float32)).astype(jnp.bfloat16).astype(jnp.float32)
        valid = (index >= 0) & (index < P_SIZE)
        clipped = jnp.clip(index, 0, P_SIZE - 1).astype(jnp.int32)
        total = total + image[:, clipped] * jnp.where(valid, taps, 0.0)[None, :]
    return total


def reference(raw, dark, flat, mask, offsets, scales, fracs):
    numerator = jnp.zeros((P_SIZE, P_SIZE), jnp.float32)
    denominator = jnp.zeros((P_SIZE, P_SIZE), jnp.float32)
    for expo in range(NEXP):
        good = mask[expo].astype(jnp.float32)
        corrected = (raw[expo].astype(jnp.float32) - dark) * flat * good
        sumsq = jnp.sum(corrected * corrected)
        count = jnp.sum(good)
        weight = count / (sumsq + 1e-5 * count)
        image16 = corrected.astype(jnp.bfloat16).astype(jnp.float32)
        colwarped = warp_last(image16, offsets[expo, 1], scales[expo, 1], fracs[expo, 1]).astype(jnp.bfloat16)
        colcover = warp_last(good, offsets[expo, 1], scales[expo, 1], fracs[expo, 1]).astype(jnp.bfloat16)
        warped = warp_last(colwarped.astype(jnp.float32).T, offsets[expo, 0], scales[expo, 0], fracs[expo, 0]).T
        cover = warp_last(colcover.astype(jnp.float32).T, offsets[expo, 0], scales[expo, 0], fracs[expo, 0]).T
        numerator = numerator + weight * warped
        denominator = denominator + weight * cover
    return numerator / jnp.maximum(denominator, 1.0)
```

```python
import functools

import jax
import jax.numpy as jnp
from jax import lax
from jax.experimental import pallas as pl
from jax.experimental.pallas import tpu as pltpu
from jax.sharding import PartitionSpec as P

MESH = pl.DeviceIdType.MESH
COL_WINDOW = 640
COL_ALIGN = 128
ROW_WINDOW = 512
ROW_ALIGN = 64


def lanczos(offsets_t):
    return jnp.where(jnp.abs(offsets_t) < 3.0, jnp.sinc(offsets_t) * jnp.sinc(offsets_t / 3.0), 0.0)


def banded(taps, first, window):
    frame = (lax.broadcasted_iota(jnp.int32, (window, taps.shape[1]), 0) + first).astype(jnp.float32)
    step = frame - taps[6:7, :]
    total = jnp.zeros_like(step)
    for tap in range(6):
        total = jnp.where(step == float(tap - 2), taps[tap : tap + 1, :], total)
    return total.astype(jnp.bfloat16)


def window_start(sky, frame_len, window, align):
    lowest = lax.div(lax.max((sky - 255) * 197 - 800, 0), 200)
    return pl.multiple_of(lax.min(lax.div(lowest, align) * align, frame_len - window), align)


def kernel(dims, raw, dark, flat, mask, taps, out, image, outgoing, stats, totals, partial, *rest):
    exposures, parts, band, frame_len, visits, n_tx, n_ty = dims
    strips = rest[:exposures]
    send_sem, recv_sem, stat_send, stat_recv, sum_send, sum_recv = rest[exposures:]
    width = frame_len // parts
    vi, ti, yi = lax.axis_index("visit"), lax.axis_index("tx"), lax.axis_index("ty")
    me = ti * n_ty + yi

    def peer(step):
        to = lax.rem(me + step, parts)
        return to, (vi, lax.div(to, n_ty), lax.rem(to, n_ty))

    barrier = pltpu.get_barrier_semaphore()

    def greet(step, carry):
        pl.semaphore_signal(barrier, inc=1, device_id=peer(step)[1], device_id_type=MESH)
        return carry

    def greet_visit(step, carry):
        to = (lax.rem(vi + step, visits), ti, yi)
        pl.semaphore_signal(barrier, inc=1, device_id=to, device_id_type=MESH)
        return carry

    lax.fori_loop(1, parts, greet, 0)
    lax.fori_loop(1, visits, greet_visit, 0)

    def correct(expo):
        def chunk(at, carry):
            sumsq, count = carry
            cols = pl.ds(pl.multiple_of(at * 128, 128), 128)
            good = mask[expo, :, cols].astype(jnp.float32)
            fixed = (raw[expo, :, cols].astype(jnp.float32) - dark[:, cols]) * flat[:, cols] * good
            image[expo, 0:band, cols] = fixed.astype(jnp.bfloat16)
            image[expo, band : 2 * band, cols] = good.astype(jnp.bfloat16)
            sumsq = sumsq + jnp.sum(fixed * fixed, axis=0, keepdims=True)
            count = count + jnp.sum(good, axis=0, keepdims=True)
            return sumsq, count

        zero = jnp.zeros((1, 128), jnp.float32)
        sumsq, count = lax.fori_loop(0, frame_len // 128, chunk, (zero, zero))
        stats[me, expo : expo + 1, :] = sumsq
        stats[me, exposures + expo : exposures + expo + 1, :] = count

    def strip_copy(expo, step):
        return pltpu.make_async_remote_copy(
            src_ref=outgoing.at[expo, step],
            dst_ref=strips[expo].at[pl.ds(pl.multiple_of(me * band, band), band), :],
            send_sem=send_sem.at[expo, step],
            recv_sem=recv_sem.at[expo, step],
            device_id=peer(step)[1],
            device_id_type=MESH,
        )

    def stat_copy(step):
        return pltpu.make_async_remote_copy(
            src_ref=stats.at[me],
            dst_ref=stats.at[me],
            send_sem=stat_send.at[step],
            recv_sem=stat_recv.at[step],
            device_id=peer(step)[1],
            device_id_type=MESH,
        )

    def column(expo, step):
        to, _ = peer(step)
        first = window_start(to * width, frame_len, COL_WINDOW, COL_ALIGN)
        cols = pl.ds(pl.multiple_of(to * width, width), width)
        k = banded(taps[expo, 1, :, cols], first, COL_WINDOW)
        operand = image[expo, :, pl.ds(first, COL_WINDOW)]
        return jnp.dot(operand, k, preferred_element_type=jnp.float32).astype(jnp.bfloat16)

    for expo in range(exposures):
        correct(expo)
        if expo == 0:
            pl.semaphore_wait(barrier, parts + visits - 2)

        def send_step(step, carry, expo=expo):
            both = column(expo, step)
            outgoing[expo, step, :, 0:width] = both[0:band]
            outgoing[expo, step, :, width : 2 * width] = both[band : 2 * band]
            strip_copy(expo, step).start()
            return carry

        lax.fori_loop(1, parts, send_step, 0)
        both = column(expo, 0)
        rows = pl.ds(pl.multiple_of(me * band, band), band)
        strips[expo][rows, 0:width] = both[0:band]
        strips[expo][rows, width : 2 * width] = both[band : 2 * band]

    def send_stat(step, carry):
        stat_copy(step).start()
        return carry

    lax.fori_loop(1, parts, send_stat, 0)

    def wait_stat(step, carry):
        stat_copy(step).wait()
        return carry

    lax.fori_loop(1, parts, wait_stat, 0)
    lanes = jnp.sum(stats[...], axis=0)
    sums = jnp.sum(lanes, axis=1, keepdims=True)

    own = frame_len // visits
    blocks = own // 128

    def sum_copy(step, block):
        to = lax.rem(vi + step, visits)
        at = pl.multiple_of(to * own + block * 128, 128)
        return pltpu.make_async_remote_copy(
            src_ref=totals.at[pl.ds(at, 128), :],
            dst_ref=partial.at[step, pl.ds(pl.multiple_of(block * 128, 128), 128), :],
            send_sem=sum_send.at[step, block],
            recv_sem=sum_recv.at[step, block],
            device_id=(to, ti, yi),
            device_id_type=MESH,
        )

    for expo in range(exposures):

        def wait_strip(step, carry, expo=expo):
            strip_copy(expo, step).wait()
            return carry

        lax.fori_loop(1, parts, wait_strip, 0)
        count = sums[exposures + expo : exposures + expo + 1, :]
        weight = count / (sums[expo : expo + 1, :] + 1e-05 * count)

        def row(at, expo=expo, weight=weight):
            at = pl.multiple_of(at, 128)
            first = window_start(at, frame_len, ROW_WINDOW, ROW_ALIGN)
            k = banded(taps[expo, 0, :, pl.ds(at, 128)], first, ROW_WINDOW)
            operand = strips[expo][pl.ds(first, ROW_WINDOW), :]
            dims_of = (((0,), (0,)), ((), ()))
            warped = weight * lax.dot_general(k, operand, dims_of, preferred_element_type=jnp.float32)
            rows = pl.ds(at, 128)
            totals[rows, :] = warped if expo == 0 else totals[rows, :] + warped

        last = expo == exposures - 1

        def row_step(index, carry, row=row, last=last):
            step, block = lax.div(index, blocks) + 1, lax.rem(index, blocks)
            row(lax.rem(vi + step, visits) * own + block * 128)
            if last:
                sum_copy(step, block).start()
            return carry

        def own_step(block, carry, row=row):
            row(vi * own + block * 128)
            return carry

        lax.fori_loop(0, (visits - 1) * blocks, row_step, 0)
        lax.fori_loop(0, blocks, own_step, 0)

    def finish(block, carry):
        rows = pl.ds(pl.multiple_of(block * 128, 128), 128)
        total = totals[pl.ds(pl.multiple_of(vi * own + block * 128, 128), 128), :]
        for step in range(1, visits):
            sum_copy(step, block).wait()
            total = total + partial[step, rows, :]
        out[rows, :] = total[:, 0:width] / jnp.maximum(total[:, width : 2 * width], 1.0)
        return carry

    lax.fori_loop(0, blocks, finish, 0)


def shards(n_visit, n_tx, n_ty, raw, dark, flat, mask, offsets, scales, fracs):
    exposures, band, frame_len = raw.shape
    parts = n_tx * n_ty
    width = frame_len // parts
    sky = jnp.arange(frame_len, dtype=jnp.float32)
    coords = (sky - offsets[..., None].astype(jnp.float32)) * scales[..., None] + fracs[..., None]
    base = jnp.floor(coords)
    near = jnp.arange(-2, 4, dtype=jnp.float32)[:, None]
    taps = lanczos(coords[:, :, None, :] - (base[:, :, None, :] + near))
    taps = taps.astype(jnp.bfloat16).astype(jnp.float32)
    taps = jnp.concatenate([taps, base[:, :, None, :], base[:, :, None, :]], axis=2)
    own = frame_len // n_visit
    vmem = pl.BlockSpec(memory_space=pltpu.VMEM)
    dims = (exposures, parts, band, frame_len, n_visit, n_tx, n_ty)
    dma = pltpu.SemaphoreType.DMA
    return pl.pallas_call(
        functools.partial(kernel, dims),
        out_shape=jax.ShapeDtypeStruct((own, width), jnp.float32),
        in_specs=[vmem] * 5,
        out_specs=vmem,
        scratch_shapes=[
            pltpu.VMEM((exposures, 2 * band, frame_len), jnp.bfloat16),
            pltpu.VMEM((exposures, parts, band, 2 * width), jnp.bfloat16),
            pltpu.VMEM((parts, 2 * exposures, 128), jnp.float32),
            pltpu.VMEM((frame_len, 2 * width), jnp.float32),
            pltpu.VMEM((n_visit, own, 2 * width), jnp.float32),
        ]
        + [pltpu.VMEM((frame_len, 2 * width), jnp.bfloat16)] * exposures
        + [
            dma((exposures, parts)),
            dma((exposures, parts)),
            dma((parts,)),
            dma((parts,)),
            dma((n_visit, own // 128)),
            dma((n_visit, own // 128)),
        ],
        compiler_params=pltpu.CompilerParams(
            collective_id=0, has_side_effects=True, vmem_limit_bytes=60000000
        ),
    )(raw, dark, flat, mask, taps)


def solution(mesh):
    in_specs = (
        P("visit", ("tx", "ty"), None),
        P(("tx", "ty"), None),
        P(("tx", "ty"), None),
        P("visit", ("tx", "ty"), None),
        P("visit", None),
        P("visit", None),
        P("visit", None),
    )
    out_specs = P("visit", ("tx", "ty"))
    body = functools.partial(shards, mesh.shape["visit"], mesh.shape["tx"], mesh.shape["ty"])
    return jax.shard_map(body, mesh=mesh, in_specs=in_specs, out_specs=out_specs, check_vma=False)
```

```python
import functools

import jax
import jax.numpy as jnp
from jax import lax
from jax.experimental import pallas as pl
from jax.experimental.pallas import tpu as pltpu
from jax.sharding import PartitionSpec as P

MESH = pl.DeviceIdType.MESH
COL_WINDOW = 640
COL_ALIGN = 128
ROW_WINDOW = 512
ROW_ALIGN = 64


def sinc(t):
    at = jnp.pi * jnp.where(t == 0.0, 1.0, t)
    return jnp.where(t == 0.0, 1.0, jnp.sin(at) / at)


def lanczos(t):
    return jnp.where(jnp.abs(t) < 3.0, sinc(t) * sinc(t / 3.0), 0.0)


def banded(taps, first, window):
    frame = (lax.broadcasted_iota(jnp.int32, (window, taps.shape[1]), 0) + first).astype(jnp.float32)
    step = frame - taps[6:7, :]
    total = jnp.zeros_like(step)
    for tap in range(6):
        total = jnp.where(step == float(tap - 2), taps[tap : tap + 1, :], total)
    return total.astype(jnp.bfloat16)


def window_start(sky, frame_len, window, align):
    lowest = lax.div(lax.max((sky - 255) * 197 - 800, 0), 200)
    return pl.multiple_of(lax.min(lax.div(lowest, align) * align, frame_len - window), align)


def kernel(dims, offsets, scales, fracs, raw_in, dark_in, flat_in, mask_in, out, *scratch):
    exposures, parts, band, frame_len, visits, n_tx, n_ty = dims
    raw, dark, flat, mask, taps, rowk, image, outgoing, stats, totals, partial = scratch[:11]
    strips = scratch[11 : 11 + exposures]
    in_sem, send_sem, recv_sem, stat_send, stat_recv, sum_send, sum_recv = scratch[11 + exposures :]
    width = frame_len // parts
    vi, ti, yi = lax.axis_index("visit"), lax.axis_index("tx"), lax.axis_index("ty")
    me = ti * n_ty + yi

    half = n_ty // 2
    own_step = parts - 1

    def peer(step):
        high, at = 1 - lax.div(step, parts // 2), lax.rem(step, parts // 2)
        low, over = lax.rem(lax.div(at, n_tx) + 1, half), lax.rem(lax.rem(at, n_tx) + 1, n_tx)
        to_y = lax.rem(lax.div(yi, half) + high, 2) * half + lax.rem(lax.rem(yi, half) + low, half)
        to_t = lax.rem(ti + over, n_tx)
        return to_t * n_ty + to_y, (vi, to_t, to_y)

    loads = [(dark_in, dark), (flat_in, flat)]
    for expo in range(exposures):
        loads += [(raw_in.at[expo], raw.at[expo]), (mask_in.at[expo], mask.at[expo])]
    loads = [pltpu.make_async_copy(src, dst, in_sem.at[n]) for n, (src, dst) in enumerate(loads)]
    for load in loads:
        load.start()

    barrier = pltpu.get_barrier_semaphore()

    def greet(step, carry):
        pl.semaphore_signal(barrier, inc=1, device_id=peer(step)[1], device_id_type=MESH)
        return carry

    def greet_visit(step, carry):
        to = (lax.rem(vi + step, visits), ti, yi)
        pl.semaphore_signal(barrier, inc=1, device_id=to, device_id_type=MESH)
        return carry

    lax.fori_loop(0, own_step, greet, 0)
    lax.fori_loop(1, visits, greet_visit, 0)

    def weigh(expo, axis):
        shape = (8, frame_len)
        sky = lax.broadcasted_iota(jnp.int32, shape, 1).astype(jnp.float32)
        tap = lax.broadcasted_iota(jnp.int32, shape, 0).astype(jnp.float32)
        offset = offsets[expo, axis].astype(jnp.float32)
        coords = (sky - offset) * scales[expo, axis] + fracs[expo, axis]
        base = jnp.floor(coords)
        values = lanczos(coords - (base + (tap - 2.0)))
        taps[expo, axis, :, :] = jnp.where(tap < 6.0, values, base)

    def correct(expo):
        def chunk(at, carry):
            sumsq, count = carry
            cols = pl.ds(pl.multiple_of(at * 128, 128), 128)
            good = mask[expo, :, cols].astype(jnp.float32)
            fixed = (raw[expo, :, cols].astype(jnp.float32) - dark[:, cols]) * flat[:, cols] * good
            image[expo, 0:band, cols] = fixed.astype(jnp.bfloat16)
            image[expo, band : 2 * band, cols] = good.astype(jnp.bfloat16)
            sumsq = sumsq + jnp.sum(fixed * fixed, axis=0, keepdims=True)
            count = count + jnp.sum(good, axis=0, keepdims=True)
            return sumsq, count

        zero = jnp.zeros((1, 128), jnp.float32)
        sumsq, count = lax.fori_loop(0, frame_len // 128, chunk, (zero, zero))
        stats[me, expo : expo + 1, :] = sumsq
        stats[me, exposures + expo : exposures + expo + 1, :] = count

    def strip_copy(expo, step):
        return pltpu.make_async_remote_copy(
            src_ref=outgoing.at[expo, step],
            dst_ref=strips[expo].at[pl.ds(pl.multiple_of(me * band, band), band), :],
            send_sem=send_sem.at[expo, step],
            recv_sem=recv_sem.at[expo, step],
            device_id=peer(step)[1],
            device_id_type=MESH,
        )

    def stat_copy(step):
        return pltpu.make_async_remote_copy(
            src_ref=stats.at[me],
            dst_ref=stats.at[me],
            send_sem=stat_send.at[step],
            recv_sem=stat_recv.at[step],
            device_id=peer(step)[1],
            device_id_type=MESH,
        )

    def column(expo, step):
        to, _ = peer(step)
        first = window_start(to * width, frame_len, COL_WINDOW, COL_ALIGN)
        cols = pl.ds(pl.multiple_of(to * width, width), width)
        k = banded(taps[expo, 1, :, cols], first, COL_WINDOW)
        operand = image[expo, :, pl.ds(first, COL_WINDOW)]
        return jnp.dot(operand, k, preferred_element_type=jnp.float32).astype(jnp.bfloat16)

    def send_stat(step, carry):
        stat_copy(step).start()
        return carry

    weigh(0, 1)
    loads[0].wait()
    loads[1].wait()
    for expo in range(exposures):
        if expo > 0:
            weigh(expo, 1)
        loads[2 + 2 * expo].wait()
        loads[3 + 2 * expo].wait()
        correct(expo)
        if expo == 0:
            pl.semaphore_wait(barrier, parts + visits - 2)
        if expo == exposures - 1:
            lax.fori_loop(0, own_step, send_stat, 0)

        def send_step(step, carry, expo=expo):
            both = column(expo, step)
            outgoing[expo, step, :, 0:width] = both[0:band]
            outgoing[expo, step, :, width : 2 * width] = both[band : 2 * band]
            strip_copy(expo, step).start()
            return carry

        lax.fori_loop(0, own_step, send_step, 0)
        both = column(expo, own_step)
        rows = pl.ds(pl.multiple_of(me * band, band), band)
        strips[expo][rows, 0:width] = both[0:band]
        strips[expo][rows, width : 2 * width] = both[band : 2 * band]

    for expo in range(exposures):
        weigh(expo, 0)

        def build(block, carry, expo=expo):
            at = pl.multiple_of(block * 128, 128)
            first = window_start(at, frame_len, ROW_WINDOW, ROW_ALIGN)
            rowk[expo, pl.ds(at, 128), :] = banded(taps[expo, 0, :, pl.ds(at, 128)], first, ROW_WINDOW).T
            return carry

        lax.fori_loop(0, frame_len // 128, build, 0)

    def wait_stat(step, carry):
        stat_copy(step).wait()
        return carry

    own = frame_len // visits
    blocks = own // 128

    def sum_copy(step, block):
        to = lax.rem(vi + step, visits)
        at = pl.multiple_of(to * own + block * 128, 128)
        return pltpu.make_async_remote_copy(
            src_ref=totals.at[pl.ds(at, 128), :],
            dst_ref=partial.at[step, pl.ds(pl.multiple_of(block * 128, 128), 128), :],
            send_sem=sum_send.at[step, block],
            recv_sem=sum_recv.at[step, block],
            device_id=(to, ti, yi),
            device_id_type=MESH,
        )

    for expo in range(exposures):

        def wait_strip(step, carry, expo=expo):
            strip_copy(expo, step).wait()
            return carry

        lax.fori_loop(0, own_step, wait_strip, 0)
        if expo == 0:
            lax.fori_loop(0, own_step, wait_stat, 0)
            lanes = jnp.sum(stats[...], axis=0)
            sums = jnp.sum(lanes, axis=1, keepdims=True)
        count = sums[exposures + expo : exposures + expo + 1, :]
        weight = count / (sums[expo : expo + 1, :] + 1e-05 * count)

        def row(at, expo=expo, weight=weight):
            at = pl.multiple_of(at, 128)
            first = window_start(at, frame_len, ROW_WINDOW, ROW_ALIGN)
            rows = pl.ds(at, 128)
            operand = strips[expo][pl.ds(first, ROW_WINDOW), :]
            k = rowk[expo, rows, :]
            warped = weight * jnp.dot(k, operand, preferred_element_type=jnp.float32)
            totals[rows, :] = warped if expo == 0 else totals[rows, :] + warped

        last = expo == exposures - 1

        def row_step(index, carry, row=row, last=last):
            step, block = lax.div(index, blocks) + 1, lax.rem(index, blocks)
            row(lax.rem(vi + step, visits) * own + block * 128)
            if last:
                sum_copy(step, block).start()
            return carry

        def own_row(block, carry, row=row):
            row(vi * own + block * 128)
            return carry

        lax.fori_loop(0, (visits - 1) * blocks, row_step, 0)
        lax.fori_loop(0, blocks, own_row, 0)

    def finish(block, carry):
        rows = pl.ds(pl.multiple_of(block * 128, 128), 128)
        total = totals[pl.ds(pl.multiple_of(vi * own + block * 128, 128), 128), :]
        for step in range(1, visits):
            sum_copy(step, block).wait()
            total = total + partial[step, rows, :]
        out[rows, :] = total[:, 0:width] / jnp.maximum(total[:, width : 2 * width], 1.0)
        return carry

    lax.fori_loop(0, blocks, finish, 0)


def shards(n_visit, n_tx, n_ty, raw, dark, flat, mask, offsets, scales, fracs):
    exposures, band, frame_len = raw.shape
    parts = n_tx * n_ty
    width = frame_len // parts
    own = frame_len // n_visit
    smem = pl.BlockSpec(memory_space=pltpu.SMEM)
    vmem = pl.BlockSpec(memory_space=pltpu.VMEM)
    dims = (exposures, parts, band, frame_len, n_visit, n_tx, n_ty)
    dma = pltpu.SemaphoreType.DMA
    return pl.pallas_call(
        functools.partial(kernel, dims),
        out_shape=jax.ShapeDtypeStruct((own, width), jnp.float32),
        in_specs=[smem] * 3 + [pl.BlockSpec(memory_space=pl.ANY)] * 4,
        out_specs=vmem,
        scratch_shapes=[
            pltpu.VMEM(raw.shape, raw.dtype),
            pltpu.VMEM(dark.shape, dark.dtype),
            pltpu.VMEM(flat.shape, flat.dtype),
            pltpu.VMEM(mask.shape, mask.dtype),
            pltpu.VMEM((exposures, 2, 8, frame_len), jnp.float32),
            pltpu.VMEM((exposures, frame_len, ROW_WINDOW), jnp.bfloat16),
            pltpu.VMEM((exposures, 2 * band, frame_len), jnp.bfloat16),
            pltpu.VMEM((exposures, parts, band, 2 * width), jnp.bfloat16),
            pltpu.VMEM((parts, 2 * exposures, 128), jnp.float32),
            pltpu.VMEM((frame_len, 2 * width), jnp.float32),
            pltpu.VMEM((n_visit, own, 2 * width), jnp.float32),
        ]
        + [pltpu.VMEM((frame_len, 2 * width), jnp.bfloat16)] * exposures
        + [
            dma((2 + 2 * exposures,)),
            dma((exposures, parts)),
            dma((exposures, parts)),
            dma((parts,)),
            dma((parts,)),
            dma((n_visit, own // 128)),
            dma((n_visit, own // 128)),
        ],
        compiler_params=pltpu.CompilerParams(
            collective_id=0, has_side_effects=True, vmem_limit_bytes=60000000
        ),
    )(offsets, scales, fracs, raw, dark, flat, mask)


def solution(mesh):
    in_specs = (
        P("visit", ("tx", "ty"), None),
        P(("tx", "ty"), None),
        P(("tx", "ty"), None),
        P("visit", ("tx", "ty"), None),
        P("visit", None),
        P("visit", None),
        P("visit", None),
    )
    out_specs = P("visit", ("tx", "ty"))
    body = functools.partial(shards, mesh.shape["visit"], mesh.shape["tx"], mesh.shape["ty"])
    return jax.shard_map(body, mesh=mesh, in_specs=in_specs, out_specs=out_specs, check_vma=False)
```

```python
import functools

import jax
import jax.numpy as jnp
from jax import lax
from jax.experimental import pallas as pl
from jax.experimental.pallas import tpu as pltpu
from jax.sharding import PartitionSpec as P

MESH = pl.DeviceIdType.MESH
COL_WINDOW = 640
COL_ALIGN = 128
ROW_WINDOW = 512
ROW_ALIGN = 64


def sinc(t):
    at = jnp.pi * jnp.where(t == 0.0, 1.0, t)
    return jnp.where(t == 0.0, 1.0, jnp.sin(at) / at)


def lanczos(t):
    return jnp.where(jnp.abs(t) < 3.0, sinc(t) * sinc(t / 3.0), 0.0)


def banded(taps, first, window):
    frame = (lax.broadcasted_iota(jnp.int32, (window, taps.shape[1]), 0) + first).astype(jnp.float32)
    step = frame - taps[6:7, :]
    total = jnp.zeros_like(step)
    for tap in range(6):
        total = jnp.where(step == float(tap - 2), taps[tap : tap + 1, :], total)
    return total.astype(jnp.bfloat16)


def window_start(sky, frame_len, window, align):
    lowest = lax.div(lax.max((sky - 255) * 197 - 800, 0), 200)
    return pl.multiple_of(lax.min(lax.div(lowest, align) * align, frame_len - window), align)


def kernel(dims, offsets, scales, fracs, raw_in, dark_in, flat_in, mask_in, out, *scratch):
    exposures, parts, band, frame_len, visits, n_tx, n_ty = dims
    raw, dark, flat, mask, taps, rowk, image, outgoing, stats, totals, partial = scratch[:11]
    strips = scratch[11 : 11 + exposures]
    in_sem, send_sem, recv_sem, stat_send, stat_recv, sum_send, sum_recv = scratch[11 + exposures :]
    width = frame_len // parts
    vi, ti, yi = lax.axis_index("visit"), lax.axis_index("tx"), lax.axis_index("ty")
    me = ti * n_ty + yi

    half = n_ty // 2
    own_step = parts - 1

    def peer(step):
        high, at = 1 - lax.div(step, parts // 2), lax.rem(step, parts // 2)
        low, over = lax.rem(lax.div(at, n_tx) + 1, half), lax.rem(lax.rem(at, n_tx) + 1, n_tx)
        to_y = lax.rem(lax.div(yi, half) + high, 2) * half + lax.rem(lax.rem(yi, half) + low, half)
        to_t = lax.rem(ti + over, n_tx)
        return to_t * n_ty + to_y, (vi, to_t, to_y)

    loads = [(dark_in, dark), (flat_in, flat)]
    for expo in range(exposures):
        loads += [(raw_in.at[expo], raw.at[expo]), (mask_in.at[expo], mask.at[expo])]
    loads = [pltpu.make_async_copy(src, dst, in_sem.at[n]) for n, (src, dst) in enumerate(loads)]
    for load in loads:
        load.start()

    barrier = pltpu.get_barrier_semaphore()

    def greet(step, carry):
        pl.semaphore_signal(barrier, inc=1, device_id=peer(step)[1], device_id_type=MESH)
        return carry

    def greet_visit(step, carry):
        to = (lax.rem(vi + step, visits), ti, yi)
        pl.semaphore_signal(barrier, inc=1, device_id=to, device_id_type=MESH)
        return carry

    lax.fori_loop(0, own_step, greet, 0)
    lax.fori_loop(1, visits, greet_visit, 0)

    def weigh(expo, axis):
        shape = (8, frame_len)
        sky = lax.broadcasted_iota(jnp.int32, shape, 1).astype(jnp.float32)
        tap = lax.broadcasted_iota(jnp.int32, shape, 0).astype(jnp.float32)
        offset = offsets[expo, axis].astype(jnp.float32)
        coords = (sky - offset) * scales[expo, axis] + fracs[expo, axis]
        base = jnp.floor(coords)
        values = lanczos(coords - (base + (tap - 2.0)))
        taps[expo, axis, :, :] = jnp.where(tap < 6.0, values, base)

    def correct(expo):
        def chunk(at, carry):
            sumsq, count = carry
            cols = pl.ds(pl.multiple_of(at * 128, 128), 128)
            good = mask[expo, :, cols].astype(jnp.float32)
            fixed = (raw[expo, :, cols].astype(jnp.float32) - dark[:, cols]) * flat[:, cols] * good
            image[expo, 0:band, cols] = fixed.astype(jnp.bfloat16)
            image[expo, band : 2 * band, cols] = good.astype(jnp.bfloat16)
            sumsq = sumsq + jnp.sum(fixed * fixed, axis=0, keepdims=True)
            count = count + jnp.sum(good, axis=0, keepdims=True)
            return sumsq, count

        zero = jnp.zeros((1, 128), jnp.float32)
        sumsq, count = lax.fori_loop(0, frame_len // 128, chunk, (zero, zero))
        stats[me, expo : expo + 1, :] = sumsq
        stats[me, exposures + expo : exposures + expo + 1, :] = count

    def strip_copy(expo, step):
        return pltpu.make_async_remote_copy(
            src_ref=outgoing.at[expo, step],
            dst_ref=strips[expo].at[pl.ds(pl.multiple_of(me * band, band), band), :],
            send_sem=send_sem.at[expo, step],
            recv_sem=recv_sem.at[expo, step],
            device_id=peer(step)[1],
            device_id_type=MESH,
        )

    def stat_copy(step):
        return pltpu.make_async_remote_copy(
            src_ref=stats.at[me],
            dst_ref=stats.at[me],
            send_sem=stat_send.at[step],
            recv_sem=stat_recv.at[step],
            device_id=peer(step)[1],
            device_id_type=MESH,
        )

    def column(expo, step):
        to, _ = peer(step)
        first = window_start(to * width, frame_len, COL_WINDOW, COL_ALIGN)
        cols = pl.ds(pl.multiple_of(to * width, width), width)
        k = banded(taps[expo, 1, :, cols], first, COL_WINDOW)
        operand = image[expo, :, pl.ds(first, COL_WINDOW)]
        return jnp.dot(operand, k, preferred_element_type=jnp.float32).astype(jnp.bfloat16)

    def send_stat(step, carry):
        stat_copy(step).start()
        return carry

    weigh(0, 1)
    loads[0].wait()
    loads[1].wait()
    for expo in range(exposures):
        if expo > 0:
            weigh(expo, 1)
        loads[2 + 2 * expo].wait()
        loads[3 + 2 * expo].wait()
        correct(expo)
        if expo == 0:
            pl.semaphore_wait(barrier, parts + visits - 2)
        if expo == exposures - 1:
            lax.fori_loop(0, own_step, send_stat, 0)

        def send_step(step, carry, expo=expo):
            step = lax.rem(step, 2) * (parts // 2) + lax.div(step, 2)
            both = column(expo, step)
            outgoing[expo, step, :, 0:width] = both[0:band]
            outgoing[expo, step, :, width : 2 * width] = both[band : 2 * band]
            strip_copy(expo, step).start()
            return carry

        lax.fori_loop(0, own_step, send_step, 0)
        both = column(expo, own_step)
        rows = pl.ds(pl.multiple_of(me * band, band), band)
        strips[expo][rows, 0:width] = both[0:band]
        strips[expo][rows, width : 2 * width] = both[band : 2 * band]

    for expo in range(exposures):
        weigh(expo, 0)

        def build(block, carry, expo=expo):
            at = pl.multiple_of(block * 128, 128)
            first = window_start(at, frame_len, ROW_WINDOW, ROW_ALIGN)
            rowk[expo, pl.ds(at, 128), :] = banded(taps[expo, 0, :, pl.ds(at, 128)], first, ROW_WINDOW).T
            return carry

        lax.fori_loop(0, frame_len // 128, build, 0)

    def wait_stat(step, carry):
        stat_copy(step).wait()
        return carry

    own = frame_len // visits
    blocks = own // 128

    def sum_copy(step, block):
        to = lax.rem(vi + step, visits)
        at = pl.multiple_of(to * own + block * 128, 128)
        return pltpu.make_async_remote_copy(
            src_ref=totals.at[pl.ds(at, 128), :],
            dst_ref=partial.at[step, pl.ds(pl.multiple_of(block * 128, 128), 128), :],
            send_sem=sum_send.at[step, block],
            recv_sem=sum_recv.at[step, block],
            device_id=(to, ti, yi),
            device_id_type=MESH,
        )

    for expo in range(exposures):

        def wait_strip(step, carry, expo=expo):
            strip_copy(expo, step).wait()
            return carry

        lax.fori_loop(0, own_step, wait_strip, 0)
        if expo == 0:
            lax.fori_loop(0, own_step, wait_stat, 0)
            lanes = jnp.sum(stats[...], axis=0)
            sums = jnp.sum(lanes, axis=1, keepdims=True)
        count = sums[exposures + expo : exposures + expo + 1, :]
        weight = count / (sums[expo : expo + 1, :] + 1e-05 * count)

        def row(at, expo=expo, weight=weight):
            at = pl.multiple_of(at, 128)
            first = window_start(at, frame_len, ROW_WINDOW, ROW_ALIGN)
            rows = pl.ds(at, 128)
            operand = strips[expo][pl.ds(first, ROW_WINDOW), :]
            k = rowk[expo, rows, :]
            warped = weight * jnp.dot(k, operand, preferred_element_type=jnp.float32)
            totals[rows, :] = warped if expo == 0 else totals[rows, :] + warped

        last = expo == exposures - 1

        def row_step(index, carry, row=row, last=last):
            step, block = lax.div(index, blocks) + 1, lax.rem(index, blocks)
            row(lax.rem(vi + step, visits) * own + block * 128)
            if last:
                sum_copy(step, block).start()
            return carry

        def own_row(block, carry, row=row):
            row(vi * own + block * 128)
            return carry

        lax.fori_loop(0, (visits - 1) * blocks, row_step, 0)
        lax.fori_loop(0, blocks, own_row, 0)

    def finish(block, carry):
        rows = pl.ds(pl.multiple_of(block * 128, 128), 128)
        total = totals[pl.ds(pl.multiple_of(vi * own + block * 128, 128), 128), :]
        for step in range(1, visits):
            sum_copy(step, block).wait()
            total = total + partial[step, rows, :]
        out[rows, :] = total[:, 0:width] / jnp.maximum(total[:, width : 2 * width], 1.0)
        return carry

    lax.fori_loop(0, blocks, finish, 0)


def shards(n_visit, n_tx, n_ty, raw, dark, flat, mask, offsets, scales, fracs):
    exposures, band, frame_len = raw.shape
    parts = n_tx * n_ty
    width = frame_len // parts
    own = frame_len // n_visit
    smem = pl.BlockSpec(memory_space=pltpu.SMEM)
    vmem = pl.BlockSpec(memory_space=pltpu.VMEM)
    dims = (exposures, parts, band, frame_len, n_visit, n_tx, n_ty)
    dma = pltpu.SemaphoreType.DMA
    return pl.pallas_call(
        functools.partial(kernel, dims),
        out_shape=jax.ShapeDtypeStruct((own, width), jnp.float32),
        in_specs=[smem] * 3 + [pl.BlockSpec(memory_space=pl.ANY)] * 4,
        out_specs=vmem,
        scratch_shapes=[
            pltpu.VMEM(raw.shape, raw.dtype),
            pltpu.VMEM(dark.shape, dark.dtype),
            pltpu.VMEM(flat.shape, flat.dtype),
            pltpu.VMEM(mask.shape, mask.dtype),
            pltpu.VMEM((exposures, 2, 8, frame_len), jnp.float32),
            pltpu.VMEM((exposures, frame_len, ROW_WINDOW), jnp.bfloat16),
            pltpu.VMEM((exposures, 2 * band, frame_len), jnp.bfloat16),
            pltpu.VMEM((exposures, parts, band, 2 * width), jnp.bfloat16),
            pltpu.VMEM((parts, 2 * exposures, 128), jnp.float32),
            pltpu.VMEM((frame_len, 2 * width), jnp.float32),
            pltpu.VMEM((n_visit, own, 2 * width), jnp.float32),
        ]
        + [pltpu.VMEM((frame_len, 2 * width), jnp.bfloat16)] * exposures
        + [
            dma((2 + 2 * exposures,)),
            dma((exposures, parts)),
            dma((exposures, parts)),
            dma((parts,)),
            dma((parts,)),
            dma((n_visit, own // 128)),
            dma((n_visit, own // 128)),
        ],
        compiler_params=pltpu.CompilerParams(
            collective_id=0, has_side_effects=True, vmem_limit_bytes=60000000
        ),
    )(offsets, scales, fracs, raw, dark, flat, mask)


def solution(mesh):
    in_specs = (
        P("visit", ("tx", "ty"), None),
        P(("tx", "ty"), None),
        P(("tx", "ty"), None),
        P("visit", ("tx", "ty"), None),
        P("visit", None),
        P("visit", None),
        P("visit", None),
    )
    out_specs = P("visit", ("tx", "ty"))
    body = functools.partial(shards, mesh.shape["visit"], mesh.shape["tx"], mesh.shape["ty"])
    return jax.shard_map(body, mesh=mesh, in_specs=in_specs, out_specs=out_specs, check_vma=False)
```

```python
import functools

import jax
import jax.numpy as jnp
from jax import lax
from jax.experimental import pallas as pl
from jax.experimental.pallas import tpu as pltpu
from jax.sharding import PartitionSpec as P

MESH = pl.DeviceIdType.MESH
COL_WINDOW = 640
COL_ALIGN = 128
ROW_WINDOW = 512
ROW_ALIGN = 64


def sinc(t):
    at = jnp.pi * jnp.where(t == 0.0, 1.0, t)
    return jnp.where(t == 0.0, 1.0, jnp.sin(at) / at)


def lanczos(t):
    return jnp.where(jnp.abs(t) < 3.0, sinc(t) * sinc(t / 3.0), 0.0)


def banded(taps, first, window):
    frame = (lax.broadcasted_iota(jnp.int32, (window, taps.shape[1]), 0) + first).astype(jnp.float32)
    step = frame - taps[6:7, :]
    total = jnp.zeros_like(step)
    for tap in range(6):
        total = jnp.where(step == float(tap - 2), taps[tap : tap + 1, :], total)
    return total.astype(jnp.bfloat16)


def window_start(sky, frame_len, window, align):
    lowest = lax.div(lax.max((sky - 255) * 197 - 800, 0), 200)
    return pl.multiple_of(lax.min(lax.div(lowest, align) * align, frame_len - window), align)


def kernel(dims, offsets, scales, fracs, raw_in, dark_in, flat_in, mask_in, out, *scratch):
    exposures, parts, band, frame_len, visits, n_tx, n_ty = dims
    raw, dark, flat, mask, taps, rowk, image, outgoing, stats, totals, partial = scratch[:11]
    strips = scratch[11 : 11 + exposures]
    in_sem, send_sem, recv_sem, stat_send, stat_recv, sum_send, sum_recv = scratch[11 + exposures :]
    width = frame_len // parts
    vi, ti, yi = lax.axis_index("visit"), lax.axis_index("tx"), lax.axis_index("ty")
    me = ti * n_ty + yi

    half = n_ty // 2
    own_step = parts - 1

    def peer(step):
        high, at = 1 - lax.div(step, parts // 2), lax.rem(step, parts // 2)
        low, over = lax.rem(lax.div(at, n_tx) + 1, half), lax.rem(lax.rem(at, n_tx) + 1, n_tx)
        to_y = lax.rem(lax.div(yi, half) + high, 2) * half + lax.rem(lax.rem(yi, half) + low, half)
        to_t = lax.rem(ti + over, n_tx)
        return to_t * n_ty + to_y, (vi, to_t, to_y)

    loads = [(dark_in, dark), (flat_in, flat)]
    for expo in range(exposures):
        loads += [(raw_in.at[expo], raw.at[expo]), (mask_in.at[expo], mask.at[expo])]
    loads = [pltpu.make_async_copy(src, dst, in_sem.at[n]) for n, (src, dst) in enumerate(loads)]
    for load in loads[:4]:
        load.start()

    barrier = pltpu.get_barrier_semaphore()

    def greet(step, carry):
        pl.semaphore_signal(barrier, inc=1, device_id=peer(step)[1], device_id_type=MESH)
        return carry

    def greet_visit(step, carry):
        to = (lax.rem(vi + step, visits), ti, yi)
        pl.semaphore_signal(barrier, inc=1, device_id=to, device_id_type=MESH)
        return carry

    lax.fori_loop(0, own_step, greet, 0)
    lax.fori_loop(1, visits, greet_visit, 0)

    def weigh(expo, axis):
        shape = (8, frame_len)
        sky = lax.broadcasted_iota(jnp.int32, shape, 1).astype(jnp.float32)
        tap = lax.broadcasted_iota(jnp.int32, shape, 0).astype(jnp.float32)
        offset = offsets[expo, axis].astype(jnp.float32)
        coords = (sky - offset) * scales[expo, axis] + fracs[expo, axis]
        base = jnp.floor(coords)
        values = lanczos(coords - (base + (tap - 2.0)))
        taps[expo, axis, :, :] = jnp.where(tap < 6.0, values, base)

    def correct(expo):
        def chunk(at, carry):
            sumsq, count = carry
            cols = pl.ds(pl.multiple_of(at * 128, 128), 128)
            good = mask[expo, :, cols].astype(jnp.float32)
            fixed = (raw[expo, :, cols].astype(jnp.float32) - dark[:, cols]) * flat[:, cols] * good
            image[expo, 0:band, cols] = fixed.astype(jnp.bfloat16)
            image[expo, band : 2 * band, cols] = good.astype(jnp.bfloat16)
            sumsq = sumsq + jnp.sum(fixed * fixed, axis=0, keepdims=True)
            count = count + jnp.sum(good, axis=0, keepdims=True)
            return sumsq, count

        zero = jnp.zeros((1, 128), jnp.float32)
        sumsq, count = lax.fori_loop(0, frame_len // 128, chunk, (zero, zero))
        stats[me, expo : expo + 1, :] = sumsq
        stats[me, exposures + expo : exposures + expo + 1, :] = count

    def strip_copy(expo, step):
        return pltpu.make_async_remote_copy(
            src_ref=outgoing.at[expo, step],
            dst_ref=strips[expo].at[pl.ds(pl.multiple_of(me * band, band), band), :],
            send_sem=send_sem.at[expo, step],
            recv_sem=recv_sem.at[expo, step],
            device_id=peer(step)[1],
            device_id_type=MESH,
        )

    def stat_copy(step):
        return pltpu.make_async_remote_copy(
            src_ref=stats.at[me],
            dst_ref=stats.at[me],
            send_sem=stat_send.at[step],
            recv_sem=stat_recv.at[step],
            device_id=peer(step)[1],
            device_id_type=MESH,
        )

    def column(expo, step):
        to, _ = peer(step)
        first = window_start(to * width, frame_len, COL_WINDOW, COL_ALIGN)
        cols = pl.ds(pl.multiple_of(to * width, width), width)
        k = banded(taps[expo, 1, :, cols], first, COL_WINDOW)
        operand = image[expo, :, pl.ds(first, COL_WINDOW)]
        return jnp.dot(operand, k, preferred_element_type=jnp.float32).astype(jnp.bfloat16)

    def send_stat(step, carry):
        stat_copy(step).start()
        return carry

    weigh(0, 1)
    loads[0].wait()
    loads[1].wait()
    for expo in range(exposures):
        if expo > 0:
            weigh(expo, 1)
        loads[2 + 2 * expo].wait()
        loads[3 + 2 * expo].wait()
        for load in loads[4 + 2 * expo : 6 + 2 * expo]:
            load.start()
        correct(expo)
        if expo == 0:
            pl.semaphore_wait(barrier, parts + visits - 2)
        if expo == exposures - 1:
            lax.fori_loop(0, own_step, send_stat, 0)

        def send_step(step, carry, expo=expo):
            step = lax.rem(step, 2) * (parts // 2) + lax.div(step, 2)
            both = column(expo, step)
            outgoing[expo, step, :, 0:width] = both[0:band]
            outgoing[expo, step, :, width : 2 * width] = both[band : 2 * band]
            strip_copy(expo, step).start()
            return carry

        lax.fori_loop(0, own_step, send_step, 0)
        both = column(expo, own_step)
        rows = pl.ds(pl.multiple_of(me * band, band), band)
        strips[expo][rows, 0:width] = both[0:band]
        strips[expo][rows, width : 2 * width] = both[band : 2 * band]

    for expo in range(exposures):
        weigh(expo, 0)

        def build(block, carry, expo=expo):
            at = pl.multiple_of(block * 128, 128)
            first = window_start(at, frame_len, ROW_WINDOW, ROW_ALIGN)
            rowk[expo, pl.ds(at, 128), :] = banded(taps[expo, 0, :, pl.ds(at, 128)], first, ROW_WINDOW).T
            return carry

        lax.fori_loop(0, frame_len // 128, build, 0)

    def wait_stat(step, carry):
        stat_copy(step).wait()
        return carry

    own = frame_len // visits
    blocks = own // 128

    def sum_copy(step, block):
        to = lax.rem(vi + step, visits)
        at = pl.multiple_of(to * own + block * 128, 128)
        return pltpu.make_async_remote_copy(
            src_ref=totals.at[pl.ds(at, 128), :],
            dst_ref=partial.at[step, pl.ds(pl.multiple_of(block * 128, 128), 128), :],
            send_sem=sum_send.at[step, block],
            recv_sem=sum_recv.at[step, block],
            device_id=(to, ti, yi),
            device_id_type=MESH,
        )

    for expo in range(exposures):

        def wait_strip(step, carry, expo=expo):
            strip_copy(expo, step).wait()
            return carry

        lax.fori_loop(0, own_step, wait_strip, 0)
        if expo == 0:
            lax.fori_loop(0, own_step, wait_stat, 0)
            lanes = jnp.sum(stats[...], axis=0)
            sums = jnp.sum(lanes, axis=1, keepdims=True)
        count = sums[exposures + expo : exposures + expo + 1, :]
        weight = count / (sums[expo : expo + 1, :] + 1e-05 * count)

        def row(at, expo=expo, weight=weight):
            at = pl.multiple_of(at, 128)
            first = window_start(at, frame_len, ROW_WINDOW, ROW_ALIGN)
            rows = pl.ds(at, 128)
            operand = strips[expo][pl.ds(first, ROW_WINDOW), :]
            k = rowk[expo, rows, :]
            warped = weight * jnp.dot(k, operand, preferred_element_type=jnp.float32)
            totals[rows, :] = warped if expo == 0 else totals[rows, :] + warped

        last = expo == exposures - 1

        def row_step(index, carry, row=row, last=last):
            step, block = lax.div(index, blocks) + 1, lax.rem(index, blocks)
            row(lax.rem(vi + step, visits) * own + block * 128)
            if last:
                sum_copy(step, block).start()
            return carry

        def own_row(block, carry, row=row):
            row(vi * own + block * 128)
            return carry

        lax.fori_loop(0, (visits - 1) * blocks, row_step, 0)
        lax.fori_loop(0, blocks, own_row, 0)

    def finish(block, carry):
        rows = pl.ds(pl.multiple_of(block * 128, 128), 128)
        total = totals[pl.ds(pl.multiple_of(vi * own + block * 128, 128), 128), :]
        for step in range(1, visits):
            sum_copy(step, block).wait()
            total = total + partial[step, rows, :]
        out[rows, :] = total[:, 0:width] / jnp.maximum(total[:, width : 2 * width], 1.0)
        return carry

    lax.fori_loop(0, blocks, finish, 0)


def shards(n_visit, n_tx, n_ty, raw, dark, flat, mask, offsets, scales, fracs):
    exposures, band, frame_len = raw.shape
    parts = n_tx * n_ty
    width = frame_len // parts
    own = frame_len // n_visit
    smem = pl.BlockSpec(memory_space=pltpu.SMEM)
    vmem = pl.BlockSpec(memory_space=pltpu.VMEM)
    dims = (exposures, parts, band, frame_len, n_visit, n_tx, n_ty)
    dma = pltpu.SemaphoreType.DMA
    return pl.pallas_call(
        functools.partial(kernel, dims),
        out_shape=jax.ShapeDtypeStruct((own, width), jnp.float32),
        in_specs=[smem] * 3 + [pl.BlockSpec(memory_space=pl.ANY)] * 4,
        out_specs=vmem,
        scratch_shapes=[
            pltpu.VMEM(raw.shape, raw.dtype),
            pltpu.VMEM(dark.shape, dark.dtype),
            pltpu.VMEM(flat.shape, flat.dtype),
            pltpu.VMEM(mask.shape, mask.dtype),
            pltpu.VMEM((exposures, 2, 8, frame_len), jnp.float32),
            pltpu.VMEM((exposures, frame_len, ROW_WINDOW), jnp.bfloat16),
            pltpu.VMEM((exposures, 2 * band, frame_len), jnp.bfloat16),
            pltpu.VMEM((exposures, parts, band, 2 * width), jnp.bfloat16),
            pltpu.VMEM((parts, 2 * exposures, 128), jnp.float32),
            pltpu.VMEM((frame_len, 2 * width), jnp.float32),
            pltpu.VMEM((n_visit, own, 2 * width), jnp.float32),
        ]
        + [pltpu.VMEM((frame_len, 2 * width), jnp.bfloat16)] * exposures
        + [
            dma((2 + 2 * exposures,)),
            dma((exposures, parts)),
            dma((exposures, parts)),
            dma((parts,)),
            dma((parts,)),
            dma((n_visit, own // 128)),
            dma((n_visit, own // 128)),
        ],
        compiler_params=pltpu.CompilerParams(
            collective_id=0, has_side_effects=True, vmem_limit_bytes=60000000
        ),
    )(offsets, scales, fracs, raw, dark, flat, mask)


def solution(mesh):
    in_specs = (
        P("visit", ("tx", "ty"), None),
        P(("tx", "ty"), None),
        P(("tx", "ty"), None),
        P("visit", ("tx", "ty"), None),
        P("visit", None),
        P("visit", None),
        P("visit", None),
    )
    out_specs = P("visit", ("tx", "ty"))
    body = functools.partial(shards, mesh.shape["visit"], mesh.shape["tx"], mesh.shape["ty"])
    return jax.shard_map(body, mesh=mesh, in_specs=in_specs, out_specs=out_specs, check_vma=False)
```
